512 devices in a mesh: seq: 32 (over z_lo, y, core), head: 16 (over x, z_hi).
Axes of the slice: x: 4, y: 8, z: 8 (z_hi: 4, z_lo: 2; z = z_hi * 2 + z_lo), core: 2. Of those that a mesh axis runs over, the one named last changes fastest.
Arguments:
- q_nope: bfloat16 [3072, 16384], P('seq', 'head'), may hold values from -6 to 6
- q_rope: bfloat16 [3072, 8192], P('seq', 'head'), may hold values from -48 to 48
- w_uk: bfloat16 [128, 128, 512], P('head'), may hold values from -0.5 to 0.5
- w_uv: bfloat16 [128, 512, 128], P('head'), may hold values from -0.25 to 0.25
- w_value: float32 [16384], P('head'), may hold values from -0.1875 to 0.1875
- kv_cache: bfloat16 [4096, 576], P('seq'), may hold values from -8 to 8
- cutoffs: int32 [3072], P('seq'), may hold values from 1 to 4096, as said below
Outputs:
- attn: bfloat16 [3072, 16384], P('seq', 'head')
- value: float32 [3072], P('seq')
The draws below stay inside these ranges and needn't reach their ends.
Inputs may be any that keep to these rules, and one draw needn't show every extreme that they name: `cutoffs`: every row sees at least the first event; some row sees the whole history and some row only the first event.
All inputs are finite; a program needn't handle non-finite values.
Results may differ from the reference program's by a relative error of at most 0.014.
Values may be sent and summed in bfloat16 or wider, within the bound.
A program may use at most 64 MiB of HBM per device.

```python
import jax
import jax.numpy as jnp
from jax import lax

LATENT = 512
ROPE = 64
NOPE = 128
VDIM = 128
HEADS = 128
ROWS = 3072
EVENTS = 4096


def draw_q_rope(key, part):
    base = jnp.clip(jax.random.normal(key, (ROWS, HEADS * ROPE), jnp.float32), -6.0, 6.0)
    return base.astype(jnp.bfloat16)


def draw_kv_cache(key, part):
    base = jnp.clip(jax.random.normal(key, (EVENTS, LATENT + ROPE), jnp.float32), -6.0, 6.0)
    return base.astype(jnp.bfloat16)


def draw_cutoffs(key, part):
    drawn = jax.random.randint(key, (ROWS,), 1, EVENTS + 1, dtype=jnp.int32)
    drawn = drawn.at[0].set(EVENTS)
    return drawn.at[1].set(1)


def block_levels(key, dims, shards, low, high):
    def one(axis_at, parts):
        draws = jax.random.uniform(jax.random.fold_in(jax.random.fold_in(key, 6), axis_at), (parts,), jnp.float32, low / len(shards), high / len(shards))
        return jnp.repeat(jnp.exp(draws), dims[axis_at] // parts).reshape((-1,) + (1,) * (len(dims) - axis_at - 1))

    gain = one(*shards[0])
    for cut in shards[1:]:
        gain = gain * one(*cut)
    return gain


def gaussian(own_key, extent, spread, reach, cuts=(), kind=jnp.bfloat16):
    entries = spread * jax.random.normal(own_key, extent, jnp.float32)
    if cuts:
        entries = entries * block_levels(own_key, extent, cuts, -0.22, 0.18)
    return jnp.clip(entries, -reach, reach).astype(kind)


def setup_inputs(seed: int = 0) -> dict:
    arg_keys = jax.random.split(jax.random.key(seed), 8)
    return {
        "q_nope": gaussian(arg_keys[0], (ROWS, HEADS * NOPE), 1.0, 6.0, ((0, 32), (1, 16))),
        "q_rope": draw_q_rope(jax.random.fold_in(arg_keys[7], 71), 0),
        "w_uk": gaussian(arg_keys[2], (HEADS, NOPE, LATENT), NOPE ** -0.5, 0.5, ((0, 16),)),
        "w_uv": gaussian(arg_keys[3], (HEADS, LATENT, VDIM), LATENT ** -0.5, 0.25, ((0, 16),)),
        "w_value": gaussian(arg_keys[4], (HEADS * VDIM,), (HEADS * VDIM // 16) ** -0.5, 0.1875, ((0, 16),), jnp.float32),
        "kv_cache": draw_kv_cache(jax.random.fold_in(arg_keys[7], 71), 0),
        "cutoffs": draw_cutoffs(jax.random.fold_in(arg_keys[7], 71), 0),
    }


softmax_scale = (128.0 + 64.0) ** -0.5


def reference(q_nope, q_rope, w_uk, w_uv, w_value, kv_cache, cutoffs):
    rows = q_nope.shape[0]
    nope_heads = q_nope.reshape(rows, HEADS, NOPE).transpose(1, 0, 2)
    rope_heads = q_rope.reshape(rows, HEADS, ROPE).transpose(1, 0, 2)
    events = jnp.arange(EVENTS, dtype=jnp.int32)
    visible = events[None, :] < cutoffs[:, None]
    latents = kv_cache[:, :LATENT]

    def one_head(pieces):
        nope_one, rope_one, uk_one, uv_one = pieces
        q_lat = jnp.dot(nope_one, uk_one, preferred_element_type=jnp.float32).astype(jnp.bfloat16)
        q_all = jnp.concatenate([q_lat, rope_one], axis=1)
        score = jnp.dot(q_all, kv_cache.T, preferred_element_type=jnp.float32) * softmax_scale
        score = jnp.where(visible, score, -jnp.inf)
        top = jnp.max(score, axis=1, keepdims=True)
        weight = jnp.exp(score - top)
        total = jnp.sum(weight, axis=1, keepdims=True)
        o_lat = jnp.dot(weight.astype(jnp.bfloat16), latents, preferred_element_type=jnp.float32) / total
        o_lat = o_lat.astype(jnp.bfloat16)
        return jnp.dot(o_lat, uv_one, preferred_element_type=jnp.float32).astype(jnp.bfloat16)

    outputs = lax.map(one_head, (nope_heads, rope_heads, w_uk, w_uv))
    attn = outputs.transpose(1, 0, 2).reshape(rows, HEADS * VDIM)
    value = jnp.sum(attn.astype(jnp.float32) * w_value[None, :], axis=1)
    return attn, value
```

```python
import jax
import jax.numpy as jnp
from jax import lax
from jax.experimental import pallas as pl
from jax.experimental.pallas import tpu as pltpu
from jax.sharding import PartitionSpec as P

MESH = pl.DeviceIdType.MESH
softmax_scale = (128.0 + 64.0) ** (-0.5)
exp2_scale = softmax_scale * 1.4426950408889634
HIDDEN = -1e30
Y, Z_HI, X = 8, 4, 4
SHARD = 128
HALF = 64
CHIP = 2 * SHARD
BLOCKS = 2


def chip_slot(plane, away):
    if away == 0:
        return plane
    if away == 4:
        return 14 + plane
    if away < 4:
        return 2 + (away - 1) * 4 + plane * 2
    return 2 + (7 - away) * 4 + plane * 2 + 1


def kernel(
    qn, qr, w_uk, w_uv, w_value, kv, cut, attn, value,
    held, q_all, accum, top, total, x_sums, z_sums,
    y_send, y_recv, z_send, z_recv, c_send, c_recv, v_send, v_recv, own_sem,
):
    rows = qn.shape[0]
    heads, _, latent = w_uk.shape
    rope = qr.shape[1] // heads
    seq, head = lax.axis_index("seq"), lax.axis_index("head")
    core = lax.rem(seq, 2)
    y = lax.rem(lax.div(seq, 2), Y)
    z_lo = lax.div(seq, 2 * Y)
    x, z_hi = lax.div(head, Z_HI), lax.rem(head, Z_HI)

    def at_y(step):
        return ((z_lo * Y + lax.rem(y + step + Y, Y)) * 2 + core, head)

    other_plane = seq + (1 - 2 * z_lo) * 2 * Y
    z_up = (other_plane, x * Z_HI + lax.rem(z_hi + z_lo, Z_HI))
    z_down = (other_plane, x * Z_HI + lax.rem(z_hi + z_lo + Z_HI - 1, Z_HI))
    twin = (seq + 1 - 2 * core, head)
    y_to = (at_y(1), at_y(-1))
    z_to = (z_up, z_down)
    x_peers = [(seq, lax.rem(x + k, X) * Z_HI + z_hi) for k in range(1, X)]
    z_peers = [(seq, x * Z_HI + lax.rem(z_hi + k, Z_HI)) for k in range(1, Z_HI)]

    barrier = pltpu.get_barrier_semaphore()
    greeted = [*y_to, *z_to, twin, *x_peers, *z_peers]
    for device in greeted:
        pl.semaphore_signal(barrier, inc=1, device_id=device, device_id_type=MESH)

    def place(slot, half=None):
        start = slot * CHIP + core * SHARD
        if half is None:
            return held.at[pl.ds(pl.multiple_of(start, SHARD), SHARD)]
        return held.at[pl.ds(pl.multiple_of(start + half * HALF, HALF), HALF)]

    def own(half):
        return kv.at[pl.ds(half * HALF, HALF)]

    def half_of(stream, unit):
        return unit % 2 if stream == 0 else 1 - unit % 2

    def away(stream, steps):
        return steps if stream == 0 else (Y - steps) % Y

    def y_copy(stream, unit):
        steps, half = unit // 2, half_of(stream, unit)
        source = own(half) if steps == 0 else place(chip_slot(0, away(stream, steps)), half)
        return pltpu.make_async_remote_copy(
            src_ref=source,
            dst_ref=place(chip_slot(0, away(stream, steps + 1)), half),
            send_sem=y_send.at[stream, unit],
            recv_sem=y_recv.at[stream, unit],
            device_id=y_to[stream],
            device_id_type=MESH,
        )

    def z_copy(stream, unit):
        if unit == 0:
            steps, half = 0, stream
            source = own(half)
        else:
            steps, half = (unit - 1) // 2 + 1, half_of(stream, unit - 1)
            source = place(chip_slot(0, away(stream, steps)), half)
        return pltpu.make_async_remote_copy(
            src_ref=source,
            dst_ref=place(chip_slot(1, away(stream, steps)), half),
            send_sem=z_send.at[stream, unit],
            recv_sem=z_recv.at[stream, unit],
            device_id=z_to[stream],
            device_id_type=MESH,
        )

    def twin_copy(index):
        if index == 0:
            source, target = kv, place(chip_slot(0, 0))
        else:
            if index < 15:
                stream, unit = (index - 1) % 2, (index - 1) // 2
                slot, half = chip_slot(0, away(stream, unit // 2 + 1)), half_of(stream, unit)
            else:
                stream, unit = (index - 15) % 2, (index - 15) // 2
                if unit == 0:
                    slot, half = chip_slot(1, 0), stream
                else:
                    slot = chip_slot(1, away(stream, (unit - 1) // 2 + 1))
                    half = half_of(stream, unit - 1)
            source = target = place(slot, half)
        return pltpu.make_async_remote_copy(
            src_ref=source,
            dst_ref=target,
            send_sem=c_send.at[index],
            recv_sem=c_recv.at[index],
            device_id=twin,
            device_id_type=MESH,
        )

    def from_y(unit):
        for stream in range(2):
            y_copy(stream, unit).wait_recv()
            if unit + 2 < 7:
                y_copy(stream, unit + 2).start()
            z_copy(stream, unit + 1).start()
            twin_copy(1 + unit * 2 + stream).start()

    def from_z(unit):
        for stream in range(2):
            z_copy(stream, unit).wait_recv()
            twin_copy(15 + unit * 2 + stream).start()

    def from_twin(*indices):
        for index in indices:
            twin_copy(index).wait_recv()

    keep_own = pltpu.make_async_copy(kv, place(chip_slot(0, 0)), own_sem)

    def first_event(plane, steps):
        z_at = lax.rem(z_lo + plane, 2)
        return (z_at * Y + lax.rem(y - steps + Y, Y)) * CHIP

    def attend(pair):
        if pair == 0:
            chips = ((0, 0), (1, 0))
        elif pair == 7:
            chips = ((0, 4), (1, 4))
        else:
            steps, plane = (pair - 1) // 2 + 1, (pair - 1) % 2
            chips = ((plane, steps), (plane, Y - steps))
        first, second = first_event(*chips[0]), first_event(*chips[1])
        size = 2 * CHIP
        column = lax.broadcasted_iota(jnp.int32, (rows, size), 1)
        event = column + jnp.where(column < CHIP, first, second - CHIP)
        bias = jnp.where(event < cut[...], 0.0, HIDDEN)
        block = held[pl.ds(pair * size, size), :]
        per = heads // BLOCKS
        for part in range(BLOCKS):
            span = pl.ds(part * per * rows, per * rows)
            score = lax.dot_general(
                q_all[span, :], block, (((1,), (1,)), ((), ())), preferred_element_type=jnp.float32
            )
            weights, scales = [], []
            for h in range(per):
                mine = pl.ds((part * per + h) * rows, rows)
                s = score[h * rows : (h + 1) * rows, :] + bias
                newest = jnp.max(s, axis=1, keepdims=True)
                if pair > 0:
                    newest = jnp.maximum(newest, top[mine, 0:1])
                    scale = jnp.exp2((top[mine, 0:1] - newest) * exp2_scale)
                    scales.append(scale)
                w = jnp.exp2((s - newest) * exp2_scale)
                added = sum(w[:, k : k + 128] for k in range(128, size, 128)) + w[:, :128]
                total[mine, :] = added if pair == 0 else total[mine, :] * scale + added
                top[mine, :] = jnp.broadcast_to(newest, (rows, 128))
                weights.append(w.astype(jnp.bfloat16))
            update = jnp.dot(
                jnp.concatenate(weights, axis=0), block[:, :latent], preferred_element_type=jnp.float32
            )
            if pair == 0:
                accum[span, :] = update
            else:
                accum[span, :] = accum[span, :] * jnp.concatenate(scales, axis=0) + update

    for h in range(heads):
        mine = pl.ds(h * rows, rows)
        q_lat = jnp.dot(qn[:, h * 128 : (h + 1) * 128], w_uk[h], preferred_element_type=jnp.float32)
        q_all[mine, :latent] = q_lat.astype(jnp.bfloat16)
        q_all[mine, latent:] = qr[:, h * rope : (h + 1) * rope]

    pl.semaphore_wait(barrier, len(greeted))
    for unit in range(2):
        for stream in range(2):
            y_copy(stream, unit).start()
            if unit == 0:
                z_copy(stream, 0).start()
    twin_copy(0).start()
    keep_own.start()

    from_y(0)
    from_z(0)
    from_y(1)
    keep_own.wait()
    from_twin(0, 15, 16)
    attend(0)
    from_y(2)
    from_z(1)
    from_z(2)
    from_twin(1, 2, 3, 4)
    attend(1)
    from_y(3)
    from_twin(17, 18, 19, 20)
    attend(2)
    from_y(4)
    from_z(3)
    from_z(4)
    from_twin(5, 6, 7, 8)
    attend(3)
    from_y(5)
    from_twin(21, 22, 23, 24)
    attend(4)
    from_y(6)
    from_z(5)
    from_z(6)
    from_twin(9, 10, 11, 12)
    attend(5)
    from_z(7)
    from_twin(25, 26, 27, 28)
    attend(6)
    from_twin(13, 14, 29, 30)
    attend(7)

    share = jnp.zeros((rows, 128), jnp.float32)
    for h in range(heads):
        mine = pl.ds(h * rows, rows)
        inverse = 1.0 / jnp.sum(total[mine, :], axis=1, keepdims=True)
        o_lat = (accum[mine, :] * inverse).astype(jnp.bfloat16)
        out = jnp.dot(o_lat, w_uv[h], preferred_element_type=jnp.float32).astype(jnp.bfloat16)
        attn[:, h * 128 : (h + 1) * 128] = out
        share = share + out.astype(jnp.float32) * w_value[h : h + 1, :]
    partial = lax.dot_general(
        jnp.ones((8, 128), jnp.float32), share, (((1,), (1,)), ((), ())),
        precision=lax.Precision.HIGHEST, preferred_element_type=jnp.float32,
    )

    def exchange(stage, sums, peers, place_here, count, mine):
        sums[0, :, :rows] = mine
        copies = [
            pltpu.make_async_remote_copy(
                src_ref=sums.at[0],
                dst_ref=sums.at[k],
                send_sem=v_send.at[stage, k],
                recv_sem=v_recv.at[stage, k],
                device_id=peers[k - 1],
                device_id_type=MESH,
            )
            for k in range(1, count)
        ]
        for copy in copies:
            copy.start()
        for copy in copies:
            copy.wait()
        result = sums[place_here, :, :rows]
        for j in range(1, count):
            result = result + sums[lax.rem(place_here - j + count, count), :, :rows]
        return result

    along_x = exchange(0, x_sums, x_peers, x, X, partial)
    value[...] = exchange(1, z_sums, z_peers, z_hi, Z_HI, along_x)

    for stream in range(2):
        for unit in range(7):
            y_copy(stream, unit).wait_send()
        for unit in range(8):
            z_copy(stream, unit).wait_send()
    for index in range(31):
        twin_copy(index).wait_send()


def on_device(q_nope, q_rope, w_uk, w_uv, w_value, kv_cache, cutoffs):
    rows = q_nope.shape[0]
    heads, _, latent = w_uk.shape
    depth = kv_cache.shape[1]
    vmem = pl.BlockSpec(memory_space=pltpu.VMEM)
    dma = pltpu.SemaphoreType.DMA
    attn, value = pl.pallas_call(
        kernel,
        out_shape=(
            jax.ShapeDtypeStruct((rows, q_nope.shape[1]), jnp.bfloat16),
            jax.ShapeDtypeStruct((8, rows), jnp.float32),
        ),
        in_specs=[vmem] * 7,
        out_specs=(vmem, vmem),
        scratch_shapes=[
            pltpu.VMEM((16 * CHIP, depth), jnp.bfloat16),
            pltpu.VMEM((heads * rows, depth), jnp.bfloat16),
            pltpu.VMEM((heads * rows, latent), jnp.float32),
            pltpu.VMEM((heads * rows, 128), jnp.float32),
            pltpu.VMEM((heads * rows, 128), jnp.float32),
            pltpu.VMEM((X, 8, 128), jnp.float32),
            pltpu.VMEM((Z_HI, 8, 128), jnp.float32),
            dma((2, 7)), dma((2, 7)), dma((2, 8)), dma((2, 8)), dma((31,)), dma((31,)),
            dma((2, 4)), dma((2, 4)), dma,
        ],
        compiler_params=pltpu.CompilerParams(
            collective_id=0, has_side_effects=True, vmem_limit_bytes=60 * 2**20
        ),
    )(q_nope, q_rope, w_uk, w_uv, w_value.reshape(heads, -1), kv_cache, cutoffs.reshape(rows, 1))
    return attn, value[0]


def solution(mesh):
    placed = (
        P("seq", "head"),
        P("seq", "head"),
        P("head", None, None),
        P("head", None, None),
        P("head"),
        P("seq", None),
        P("seq"),
    )
    return jax.shard_map(
        on_device,
        mesh=mesh,
        in_specs=placed,
        out_specs=(P("seq", "head"), P("seq")),
        check_vma=False,
    )
```

```python
import jax
import jax.numpy as jnp
from jax import lax
from jax.experimental import pallas as pl
from jax.experimental.pallas import tpu as pltpu
from jax.sharding import PartitionSpec as P

MESH = pl.DeviceIdType.MESH
softmax_scale = (128.0 + 64.0) ** (-0.5)
exp2_scale = softmax_scale * 1.4426950408889634
HIDDEN = -1e30
Y, Z_HI, X = 8, 4, 4
SHARD = 128
CHIP = 2 * SHARD
BLOCKS = 1


def chip_slot(plane, away):
    if away == 0:
        return plane
    if away == 4:
        return 14 + plane
    if away < 4:
        return 2 + (away - 1) * 4 + plane * 2
    return 2 + (7 - away) * 4 + plane * 2 + 1


def kernel(
    qn_in, qr_in, w_uk_in, w_uv_in, w_value, kv, cut, attn, value,
    qn, qr, w_uk, w_uv, held, q_all, accum, top, total, x_sums, z_sums,
    y_send, y_recv, z_send, z_recv, c_send, c_recv, v_send, v_recv, in_sem,
):
    rows = qn.shape[0]
    heads, _, latent = w_uk.shape
    rope = qr.shape[1] // heads
    seq, head = lax.axis_index("seq"), lax.axis_index("head")
    core = lax.rem(seq, 2)
    y = lax.rem(lax.div(seq, 2), Y)
    z_lo = lax.div(seq, 2 * Y)
    x, z_hi = lax.div(head, Z_HI), lax.rem(head, Z_HI)

    def at_y(step):
        return ((z_lo * Y + lax.rem(y + step + Y, Y)) * 2 + core, head)

    other_plane = seq + (1 - 2 * z_lo) * 2 * Y
    z_up = (other_plane, x * Z_HI + lax.rem(z_hi + z_lo, Z_HI))
    z_down = (other_plane, x * Z_HI + lax.rem(z_hi + z_lo + Z_HI - 1, Z_HI))
    twin = (seq + 1 - 2 * core, head)
    y_to = (at_y(1), at_y(-1))
    z_to = (z_up, z_down)
    x_peers = [(seq, lax.rem(x + k, X) * Z_HI + z_hi) for k in range(1, X)]
    z_peers = [(seq, x * Z_HI + lax.rem(z_hi + k, Z_HI)) for k in range(1, Z_HI)]

    barrier = pltpu.get_barrier_semaphore()
    greeted = [*y_to, *z_to, twin, *x_peers, *z_peers]
    for device in greeted:
        pl.semaphore_signal(barrier, inc=1, device_id=device, device_id_type=MESH)

    part_depth = kv.shape[0] // 2

    def place(slot, half=None):
        if half is None:
            return held.at[slot * 2 + core]
        return held.at[slot * 2 + core, pl.ds(half * part_depth, part_depth)]

    def own(half):
        return kv.at[pl.ds(half * part_depth, part_depth)]

    def half_of(stream, unit):
        return unit % 2 if stream == 0 else 1 - unit % 2

    def away(stream, steps):
        return steps if stream == 0 else (Y - steps) % Y

    def y_copy(stream, unit):
        steps, half = unit // 2, half_of(stream, unit)
        source = own(half) if steps == 0 else place(chip_slot(0, away(stream, steps)), half)
        return pltpu.make_async_remote_copy(
            src_ref=source,
            dst_ref=place(chip_slot(0, away(stream, steps + 1)), half),
            send_sem=y_send.at[stream, unit],
            recv_sem=y_recv.at[stream, unit],
            device_id=y_to[stream],
            device_id_type=MESH,
        )

    def z_copy(stream, unit):
        if unit == 0:
            steps, half = 0, stream
            source = own(half)
        else:
            steps, half = (unit - 1) // 2 + 1, half_of(stream, unit - 1)
            source = place(chip_slot(0, away(stream, steps)), half)
        return pltpu.make_async_remote_copy(
            src_ref=source,
            dst_ref=place(chip_slot(1, away(stream, steps)), half),
            send_sem=z_send.at[stream, unit],
            recv_sem=z_recv.at[stream, unit],
            device_id=z_to[stream],
            device_id_type=MESH,
        )

    def twin_copy(index):
        if index == 0:
            source, target = kv, place(chip_slot(0, 0))
        else:
            if index < 15:
                stream, unit = (index - 1) % 2, (index - 1) // 2
                slot, half = chip_slot(0, away(stream, unit // 2 + 1)), half_of(stream, unit)
            else:
                stream, unit = (index - 15) % 2, (index - 15) // 2
                if unit == 0:
                    slot, half = chip_slot(1, 0), stream
                else:
                    slot = chip_slot(1, away(stream, (unit - 1) // 2 + 1))
                    half = half_of(stream, unit - 1)
            source = target = place(slot, half)
        return pltpu.make_async_remote_copy(
            src_ref=source,
            dst_ref=target,
            send_sem=c_send.at[index],
            recv_sem=c_recv.at[index],
            device_id=twin,
            device_id_type=MESH,
        )

    def from_y(unit):
        for stream in range(2):
            y_copy(stream, unit).wait_recv()
            if unit + 2 < 7:
                y_copy(stream, unit + 2).start()
            z_copy(stream, unit + 1).start()
            twin_copy(1 + unit * 2 + stream).start()

    def from_z(unit):
        for stream in range(2):
            z_copy(stream, unit).wait_recv()
            twin_copy(15 + unit * 2 + stream).start()

    def from_twin(*indices):
        for index in indices:
            twin_copy(index).wait_recv()


    def first_event(plane, steps):
        z_at = lax.rem(z_lo + plane, 2)
        return (z_at * Y + lax.rem(y - steps + Y, Y)) * CHIP

    def attend(pair):
        if pair == 0:
            chips = ((0, 0), (1, 0))
        elif pair == 7:
            chips = ((0, 4), (1, 4))
        else:
            steps, plane = (pair - 1) // 2 + 1, (pair - 1) % 2
            chips = ((plane, steps), (plane, Y - steps))
        first, second = first_event(*chips[0]), first_event(*chips[1])
        size = 2 * CHIP
        column = lax.broadcasted_iota(jnp.int32, (rows, size), 1)
        event = column + jnp.where(column < CHIP, first, second - CHIP)
        bias = jnp.where(event < visible, 0.0, HIDDEN)
        block = jnp.concatenate([held[pair * 4 + k] for k in range(4)], axis=1)
        per = heads // BLOCKS
        for part in range(BLOCKS):
            span = pl.ds(part * per * rows, per * rows)
            score = jnp.dot(q_all[span, :], block, preferred_element_type=jnp.float32)
            weights, scales = [], []
            for h in range(per):
                mine = pl.ds((part * per + h) * rows, rows)
                s = score[h * rows : (h + 1) * rows, :] + bias
                newest = jnp.max(s, axis=1, keepdims=True)
                if pair > 0:
                    newest = jnp.maximum(newest, top[mine, 0:1])
                    scale = jnp.exp2((top[mine, 0:1] - newest) * exp2_scale)
                    scales.append(scale)
                w = jnp.exp2((s - newest) * exp2_scale)
                added = sum(w[:, k : k + 128] for k in range(128, size, 128)) + w[:, :128]
                total[mine, :] = added if pair == 0 else total[mine, :] * scale + added
                top[mine, :] = jnp.broadcast_to(newest, (rows, 128))
                weights.append(w.astype(jnp.bfloat16))
            update = lax.dot_general(
                jnp.concatenate(weights, axis=0), block[:latent], (((1,), (1,)), ((), ())),
                preferred_element_type=jnp.float32,
            )
            if pair == 0:
                accum[span, :] = update
            else:
                accum[span, :] = accum[span, :] * jnp.concatenate(scales, axis=0) + update

    fetches = [
        pltpu.make_async_copy(source, target, in_sem.at[k])
        for k, (source, target) in enumerate(
            ((qn_in, qn), (w_uk_in, w_uk), (qr_in, qr), (kv, place(chip_slot(0, 0))), (w_uv_in, w_uv))
        )
    ]
    for fetch in fetches:
        fetch.start()
    square = (rows, rows)
    on_diagonal = lax.broadcasted_iota(jnp.int32, square, 0) == lax.broadcasted_iota(jnp.int32, square, 1)
    as_row = jnp.broadcast_to(cut[...].astype(jnp.float32), square)
    visible = jnp.sum(jnp.where(on_diagonal, as_row, 0.0), axis=1, keepdims=True).astype(jnp.int32)

    pl.semaphore_wait(barrier, len(greeted))
    for unit in range(2):
        for stream in range(2):
            y_copy(stream, unit).start()
            if unit == 0:
                z_copy(stream, 0).start()
    twin_copy(0).start()

    for fetch in fetches[:3]:
        fetch.wait()
    for h in range(heads):
        mine = pl.ds(h * rows, rows)
        q_lat = jnp.dot(qn[:, h * 128 : (h + 1) * 128], w_uk[h], preferred_element_type=jnp.float32)
        q_all[mine, :latent] = q_lat.astype(jnp.bfloat16)
        q_all[mine, latent:] = qr[:, h * rope : (h + 1) * rope]

    from_y(0)
    from_z(0)
    from_y(1)
    fetches[3].wait()
    from_twin(0, 15, 16)
    attend(0)
    from_y(2)
    from_z(1)
    from_z(2)
    from_twin(1, 2, 3, 4)
    attend(1)
    from_y(3)
    from_twin(17, 18, 19, 20)
    attend(2)
    from_y(4)
    from_z(3)
    from_z(4)
    from_twin(5, 6, 7, 8)
    attend(3)
    from_y(5)
    from_twin(21, 22, 23, 24)
    attend(4)
    from_y(6)
    from_z(5)
    from_z(6)
    from_twin(9, 10, 11, 12)
    attend(5)
    from_z(7)
    from_twin(25, 26, 27, 28)
    attend(6)
    from_twin(13, 14, 29, 30)
    attend(7)

    fetches[4].wait()
    share = jnp.zeros((rows, 128), jnp.float32)
    for h in range(heads):
        mine = pl.ds(h * rows, rows)
        inverse = 1.0 / jnp.sum(total[mine, :], axis=1, keepdims=True)
        o_lat = (accum[mine, :] * inverse).astype(jnp.bfloat16)
        out = jnp.dot(o_lat, w_uv[h], preferred_element_type=jnp.float32).astype(jnp.bfloat16)
        attn[:, h * 128 : (h + 1) * 128] = out
        share = share + out.astype(jnp.float32) * w_value[h : h + 1, :]
    partial = lax.dot_general(
        jnp.ones((8, 128), jnp.float32), share, (((1,), (1,)), ((), ())),
        precision=lax.Precision.HIGHEST, preferred_element_type=jnp.float32,
    )

    def exchange(stage, sums, peers, place_here, count, mine):
        sums[0, :, :rows] = mine
        copies = [
            pltpu.make_async_remote_copy(
                src_ref=sums.at[0],
                dst_ref=sums.at[k],
                send_sem=v_send.at[stage, k],
                recv_sem=v_recv.at[stage, k],
                device_id=peers[k - 1],
                device_id_type=MESH,
            )
            for k in range(1, count)
        ]
        for copy in copies:
            copy.start()
        for copy in copies:
            copy.wait()
        result = sums[place_here, :, :rows]
        for j in range(1, count):
            result = result + sums[lax.rem(place_here - j + count, count), :, :rows]
        return result

    along_x = exchange(0, x_sums, x_peers, x, X, partial)
    value[...] = exchange(1, z_sums, z_peers, z_hi, Z_HI, along_x)[:1]

    for stream in range(2):
        for unit in range(7):
            y_copy(stream, unit).wait_send()
        for unit in range(8):
            z_copy(stream, unit).wait_send()
    for index in range(31):
        twin_copy(index).wait_send()


def on_device(q_nope, q_rope, w_uk, w_uv, w_value, kv_cache, cutoffs):
    rows = q_nope.shape[0]
    heads, _, latent = w_uk.shape
    depth = kv_cache.shape[1]
    place = pl.BlockSpec(memory_space=pl.ANY)
    vmem = pl.BlockSpec(memory_space=pltpu.VMEM)
    dma = pltpu.SemaphoreType.DMA
    attn, value = pl.pallas_call(
        kernel,
        out_shape=(
            jax.ShapeDtypeStruct((rows, q_nope.shape[1]), jnp.bfloat16),
            jax.ShapeDtypeStruct((1, rows), jnp.float32),
        ),
        in_specs=[place] * 4 + [vmem, place, vmem],
        out_specs=(vmem, vmem),
        scratch_shapes=[
            pltpu.VMEM(q_nope.shape, jnp.bfloat16),
            pltpu.VMEM(q_rope.shape, jnp.bfloat16),
            pltpu.VMEM(w_uk.shape, jnp.bfloat16),
            pltpu.VMEM(w_uv.shape, jnp.bfloat16),
            pltpu.VMEM((32, depth, SHARD), jnp.bfloat16),
            pltpu.VMEM((heads * rows, depth), jnp.bfloat16),
            pltpu.VMEM((heads * rows, latent), jnp.float32),
            pltpu.VMEM((heads * rows, 128), jnp.float32),
            pltpu.VMEM((heads * rows, 128), jnp.float32),
            pltpu.VMEM((X, 8, 128), jnp.float32),
            pltpu.VMEM((Z_HI, 8, 128), jnp.float32),
            dma((2, 7)), dma((2, 7)), dma((2, 8)), dma((2, 8)), dma((31,)), dma((31,)),
            dma((2, 4)), dma((2, 4)), dma((5,)),
        ],
        compiler_params=pltpu.CompilerParams(
            collective_id=0, has_side_effects=True, vmem_limit_bytes=60 * 2**20
        ),
    )(q_nope, q_rope, w_uk, w_uv, w_value.reshape(heads, -1), kv_cache.T, cutoffs.reshape(1, rows))
    return attn, value.reshape(rows)


def solution(mesh):
    placed = (
        P("seq", "head"),
        P("seq", "head"),
        P("head", None, None),
        P("head", None, None),
        P("head"),
        P("seq", None),
        P("seq"),
    )
    return jax.shard_map(
        on_device,
        mesh=mesh,
        in_specs=placed,
        out_specs=(P("seq", "head"), P("seq")),
        check_vma=False,
    )
```

```python
import jax
import jax.numpy as jnp
from jax import lax
from jax.experimental import pallas as pl
from jax.experimental.pallas import tpu as pltpu
from jax.sharding import PartitionSpec as P

MESH = pl.DeviceIdType.MESH
softmax_scale = (128.0 + 64.0) ** (-0.5)
exp2_scale = softmax_scale * 1.4426950408889634
HIDDEN = -1e30
Y, Z_HI, X = 8, 4, 4
SHARD = 128
CHIP = 2 * SHARD
BLOCKS = 1


def chip_slot(plane, away):
    if away == 0:
        return plane
    if away == 4:
        return 14 + plane
    if away < 4:
        return 2 + (away - 1) * 4 + plane * 2
    return 2 + (7 - away) * 4 + plane * 2 + 1


def kernel(
    qn_in, qr_in, w_uk_in, w_uv_in, w_value, kv, cut, attn, value,
    qn, qr, w_uk, w_uv, held, q_all, accum, top, total, x_sums, z_sums,
    y_send, y_recv, z_send, z_recv, x_send, x_recv, c_send, c_recv, v_send, v_recv, in_sem,
):
    rows = qn.shape[0]
    heads, _, latent = w_uk.shape
    rope = qr.shape[1] // heads
    seq, head = lax.axis_index("seq"), lax.axis_index("head")
    core = lax.rem(seq, 2)
    y = lax.rem(lax.div(seq, 2), Y)
    z_lo = lax.div(seq, 2 * Y)
    x, z_hi = lax.div(head, Z_HI), lax.rem(head, Z_HI)

    def at_y(step):
        return ((z_lo * Y + lax.rem(y + step + Y, Y)) * 2 + core, head)

    other_plane = seq + (1 - 2 * z_lo) * 2 * Y
    z_up = (other_plane, x * Z_HI + lax.rem(z_hi + z_lo, Z_HI))
    z_down = (other_plane, x * Z_HI + lax.rem(z_hi + z_lo + Z_HI - 1, Z_HI))
    twin = (seq + 1 - 2 * core, head)
    y_to = (at_y(1), at_y(-1))
    z_to = (z_up, z_down)
    x_peers = [(seq, lax.rem(x + k, X) * Z_HI + z_hi) for k in range(1, X)]
    z_peers = [(seq, x * Z_HI + lax.rem(z_hi + k, Z_HI)) for k in range(1, Z_HI)]

    barrier = pltpu.get_barrier_semaphore()
    greeted = [*y_to, *z_to, twin, *x_peers, *z_peers]
    for device in greeted:
        pl.semaphore_signal(barrier, inc=1, device_id=device, device_id_type=MESH)

    third = kv.shape[0] // 3
    odd = lax.rem(x, 2)
    piece_at = (0, third * (1 + odd), third * (2 - odd))

    def rows_of(piece):
        start = piece_at[piece]
        return pl.ds(start if piece == 0 else pl.multiple_of(start, third), third)

    def place(slot, piece=None):
        if piece is None:
            return held.at[slot * 2 + core]
        return held.at[slot * 2 + core, rows_of(piece)]

    def own(piece):
        return kv.at[rows_of(piece)]

    def half_of(stream, unit):
        return unit % 2 if stream == 0 else 1 - unit % 2

    def away(stream, steps):
        return steps if stream == 0 else (Y - steps) % Y

    def y_copy(stream, unit):
        steps, half = unit // 2, half_of(stream, unit)
        source = own(half) if steps == 0 else place(chip_slot(0, away(stream, steps)), half)
        return pltpu.make_async_remote_copy(
            src_ref=source,
            dst_ref=place(chip_slot(0, away(stream, steps + 1)), half),
            send_sem=y_send.at[stream, unit],
            recv_sem=y_recv.at[stream, unit],
            device_id=y_to[stream],
            device_id_type=MESH,
        )

    def z_copy(stream, unit):
        if unit == 0:
            steps, half = 0, stream
            source = own(half)
        else:
            steps, half = (unit - 1) // 2 + 1, half_of(stream, unit - 1)
            source = place(chip_slot(0, away(stream, steps)), half)
        return pltpu.make_async_remote_copy(
            src_ref=source,
            dst_ref=place(chip_slot(1, away(stream, steps)), half),
            send_sem=z_send.at[stream, unit],
            recv_sem=z_recv.at[stream, unit],
            device_id=z_to[stream],
            device_id_type=MESH,
        )

    def x_slot(index):
        unit = index if index < 7 else index - 8
        if unit < 0:
            return chip_slot(1, 0), 1
        stream, steps = (0 if unit % 2 else 1), unit // 2 + 1
        return chip_slot(index // 7 if index < 14 else 1, away(stream, steps)), 1 if stream == 1 and steps < 4 else 0

    def x_copy(index):
        slot, down = x_slot(index)
        return pltpu.make_async_remote_copy(
            src_ref=place(slot, 1),
            dst_ref=place(slot, 1),
            send_sem=x_send.at[index],
            recv_sem=x_recv.at[index],
            device_id=x_peers[X - 2 if down else 0],
            device_id_type=MESH,
        )

    def twin_copy(index):
        if index == 0:
            source, target = kv, place(chip_slot(0, 0))
        elif index > 30:
            source = target = place(x_slot(index - 31)[0], 2)
        else:
            if index < 15:
                stream, unit = (index - 1) % 2, (index - 1) // 2
                slot, half = chip_slot(0, away(stream, unit // 2 + 1)), half_of(stream, unit)
            else:
                stream, unit = (index - 15) % 2, (index - 15) // 2
                if unit == 0:
                    slot, half = chip_slot(1, 0), stream
                else:
                    slot = chip_slot(1, away(stream, (unit - 1) // 2 + 1))
                    half = half_of(stream, unit - 1)
            source = target = place(slot, half)
        return pltpu.make_async_remote_copy(
            src_ref=source,
            dst_ref=target,
            send_sem=c_send.at[index],
            recv_sem=c_recv.at[index],
            device_id=twin,
            device_id_type=MESH,
        )

    def from_y(unit):
        for stream in range(2):
            y_copy(stream, unit).wait_recv()
            if unit + 2 < 7:
                y_copy(stream, unit + 2).start()
            z_copy(stream, unit + 1).start()
            twin_copy(1 + unit * 2 + stream).start()
            if half_of(stream, unit) == 1:
                x_copy(unit).start()

    def from_z(unit):
        for stream in range(2):
            z_copy(stream, unit).wait_recv()
            twin_copy(15 + unit * 2 + stream).start()
            if (stream if unit == 0 else half_of(stream, unit - 1)) == 1:
                x_copy(7 + unit).start()

    def from_x(*indices):
        for index in indices:
            x_copy(index).wait_recv()
            twin_copy(31 + index).start()

    def from_twin(*indices):
        for index in indices:
            twin_copy(index).wait_recv()


    def first_event(plane, steps):
        z_at = lax.rem(z_lo + plane, 2)
        return (z_at * Y + lax.rem(y - steps + Y, Y)) * CHIP

    def attend(pair):
        if pair == 0:
            chips = ((0, 0), (1, 0))
        elif pair == 7:
            chips = ((0, 4), (1, 4))
        else:
            steps, plane = (pair - 1) // 2 + 1, (pair - 1) % 2
            chips = ((plane, steps), (plane, Y - steps))
        first, second = first_event(*chips[0]), first_event(*chips[1])
        size = 2 * CHIP
        column = lax.broadcasted_iota(jnp.int32, (rows, size), 1)
        event = column + jnp.where(column < CHIP, first, second - CHIP)
        bias = jnp.where(event < visible, 0.0, HIDDEN)
        block = jnp.concatenate([held[pair * 4 + k] for k in range(4)], axis=1)
        per = heads // BLOCKS
        for part in range(BLOCKS):
            span = pl.ds(part * per * rows, per * rows)
            score = jnp.dot(q_all[span, :], block, preferred_element_type=jnp.float32)
            weights, scales = [], []
            for h in range(per):
                mine = pl.ds((part * per + h) * rows, rows)
                s = score[h * rows : (h + 1) * rows, :] + bias
                newest = jnp.max(s, axis=1, keepdims=True)
                if pair > 0:
                    newest = jnp.maximum(newest, top[mine, 0:1])
                    scale = jnp.exp2((top[mine, 0:1] - newest) * exp2_scale)
                    scales.append(scale)
                w = jnp.exp2((s - newest) * exp2_scale)
                added = sum(w[:, k : k + 128] for k in range(128, size, 128)) + w[:, :128]
                total[mine, :] = added if pair == 0 else total[mine, :] * scale + added
                top[mine, :] = jnp.broadcast_to(newest, (rows, 128))
                weights.append(w.astype(jnp.bfloat16))
            update = lax.dot_general(
                jnp.concatenate(weights, axis=0), block[:latent], (((1,), (1,)), ((), ())),
                preferred_element_type=jnp.float32,
            )
            if pair == 0:
                accum[span, :] = update
            else:
                accum[span, :] = accum[span, :] * jnp.concatenate(scales, axis=0) + update

    fetches = [
        pltpu.make_async_copy(source, target, in_sem.at[k])
        for k, (source, target) in enumerate(
            ((qn_in, qn), (w_uk_in, w_uk), (qr_in, qr), (kv, place(chip_slot(0, 0))), (w_uv_in, w_uv))
        )
    ]
    for fetch in fetches:
        fetch.start()
    square = (rows, rows)
    on_diagonal = lax.broadcasted_iota(jnp.int32, square, 0) == lax.broadcasted_iota(jnp.int32, square, 1)
    as_row = jnp.broadcast_to(cut[...].astype(jnp.float32), square)
    visible = jnp.sum(jnp.where(on_diagonal, as_row, 0.0), axis=1, keepdims=True).astype(jnp.int32)

    pl.semaphore_wait(barrier, len(greeted))
    for unit in range(2):
        for stream in range(2):
            y_copy(stream, unit).start()
            if unit == 0:
                z_copy(stream, 0).start()
    twin_copy(0).start()

    for fetch in fetches[:3]:
        fetch.wait()
    for h in range(heads):
        mine = pl.ds(h * rows, rows)
        q_lat = jnp.dot(qn[:, h * 128 : (h + 1) * 128], w_uk[h], preferred_element_type=jnp.float32)
        q_all[mine, :latent] = q_lat.astype(jnp.bfloat16)
        q_all[mine, latent:] = qr[:, h * rope : (h + 1) * rope]

    from_y(0)
    from_z(0)
    from_y(1)
    from_z(1)
    fetches[3].wait()
    from_x(7)
    from_twin(0, 15, 16, 38)
    attend(0)
    from_y(2)
    from_z(2)
    from_x(0, 1)
    from_y(3)
    from_twin(1, 2, 3, 4, 31, 32)
    attend(1)
    from_z(3)
    from_x(8, 9)
    from_y(4)
    from_twin(17, 18, 19, 20, 39, 40)
    attend(2)
    from_y(5)
    from_z(4)
    from_x(2, 3)
    from_twin(5, 6, 7, 8, 33, 34)
    attend(3)
    from_y(6)
    from_z(5)
    from_x(10, 11)
    from_twin(21, 22, 23, 24, 41, 42)
    attend(4)
    from_z(6)
    from_z(7)
    from_x(4, 5)
    from_twin(9, 10, 11, 12, 35, 36)
    attend(5)
    from_x(12, 13, 6, 14)
    from_twin(25, 26, 27, 28, 43, 44)
    attend(6)
    from_twin(13, 14, 29, 30, 37, 45)
    attend(7)

    fetches[4].wait()
    share = jnp.zeros((rows, 128), jnp.float32)
    for h in range(heads):
        mine = pl.ds(h * rows, rows)
        inverse = 1.0 / jnp.sum(total[mine, :], axis=1, keepdims=True)
        o_lat = (accum[mine, :] * inverse).astype(jnp.bfloat16)
        out = jnp.dot(o_lat, w_uv[h], preferred_element_type=jnp.float32).astype(jnp.bfloat16)
        attn[:, h * 128 : (h + 1) * 128] = out
        share = share + out.astype(jnp.float32) * w_value[h : h + 1, :]
    partial = lax.dot_general(
        jnp.ones((8, 128), jnp.float32), share, (((1,), (1,)), ((), ())),
        precision=lax.Precision.HIGHEST, preferred_element_type=jnp.float32,
    )

    def exchange(stage, sums, peers, place_here, count, mine):
        sums[0, :, :rows] = mine
        copies = [
            pltpu.make_async_remote_copy(
                src_ref=sums.at[0],
                dst_ref=sums.at[k],
                send_sem=v_send.at[stage, k],
                recv_sem=v_recv.at[stage, k],
                device_id=peers[k - 1],
                device_id_type=MESH,
            )
            for k in range(1, count)
        ]
        for copy in copies:
            copy.start()
        for copy in copies:
            copy.wait()
        result = sums[place_here, :, :rows]
        for j in range(1, count):
            result = result + sums[lax.rem(place_here - j + count, count), :, :rows]
        return result

    along_x = exchange(0, x_sums, x_peers, x, X, partial)
    value[...] = exchange(1, z_sums, z_peers, z_hi, Z_HI, along_x)[:1]

    for stream in range(2):
        for unit in range(7):
            y_copy(stream, unit).wait_send()
        for unit in range(8):
            z_copy(stream, unit).wait_send()
    for index in range(15):
        x_copy(index).wait_send()
    for index in range(46):
        twin_copy(index).wait_send()


def on_device(q_nope, q_rope, w_uk, w_uv, w_value, kv_cache, cutoffs):
    rows = q_nope.shape[0]
    heads, _, latent = w_uk.shape
    depth = kv_cache.shape[1]
    place = pl.BlockSpec(memory_space=pl.ANY)
    vmem = pl.BlockSpec(memory_space=pltpu.VMEM)
    dma = pltpu.SemaphoreType.DMA
    attn, value = pl.pallas_call(
        kernel,
        out_shape=(
            jax.ShapeDtypeStruct((rows, q_nope.shape[1]), jnp.bfloat16),
            jax.ShapeDtypeStruct((1, rows), jnp.float32),
        ),
        in_specs=[place] * 4 + [vmem, place, vmem],
        out_specs=(vmem, vmem),
        scratch_shapes=[
            pltpu.VMEM(q_nope.shape, jnp.bfloat16),
            pltpu.VMEM(q_rope.shape, jnp.bfloat16),
            pltpu.VMEM(w_uk.shape, jnp.bfloat16),
            pltpu.VMEM(w_uv.shape, jnp.bfloat16),
            pltpu.VMEM((32, depth, SHARD), jnp.bfloat16),
            pltpu.VMEM((heads * rows, depth), jnp.bfloat16),
            pltpu.VMEM((heads * rows, latent), jnp.float32),
            pltpu.VMEM((heads * rows, 128), jnp.float32),
            pltpu.VMEM((heads * rows, 128), jnp.float32),
            pltpu.VMEM((X, 8, 128), jnp.float32),
            pltpu.VMEM((Z_HI, 8, 128), jnp.float32),
            dma((2, 7)), dma((2, 7)), dma((2, 8)), dma((2, 8)), dma((15,)), dma((15,)), dma((46,)), dma((46,)),
            dma((2, 4)), dma((2, 4)), dma((5,)),
        ],
        compiler_params=pltpu.CompilerParams(
            collective_id=0, has_side_effects=True, vmem_limit_bytes=60 * 2**20
        ),
    )(q_nope, q_rope, w_uk, w_uv, w_value.reshape(heads, -1), kv_cache.T, cutoffs.reshape(1, rows))
    return attn, value.reshape(rows)


def solution(mesh):
    placed = (
        P("seq", "head"),
        P("seq", "head"),
        P("head", None, None),
        P("head", None, None),
        P("head"),
        P("seq", None),
        P("seq"),
    )
    return jax.shard_map(
        on_device,
        mesh=mesh,
        in_specs=placed,
        out_specs=(P("seq", "head"), P("seq")),
        check_vma=False,
    )
```

```python
import jax
import jax.numpy as jnp
from jax import lax
from jax.experimental import pallas as pl
from jax.experimental.pallas import tpu as pltpu
from jax.sharding import PartitionSpec as P

MESH = pl.DeviceIdType.MESH
softmax_scale = (128.0 + 64.0) ** (-0.5)
exp2_scale = softmax_scale * 1.4426950408889634
HIDDEN = -1e30
Y, Z_HI, X = 8, 4, 4
SHARD = 128
CHIP = 2 * SHARD
BLOCKS = 1


def chip_slot(plane, away):
    if away == 0:
        return plane
    if away == 4:
        return 14 + plane
    if away < 4:
        return 2 + (away - 1) * 4 + plane * 2
    return 2 + (7 - away) * 4 + plane * 2 + 1


def kernel(
    qn_in, qr_in, w_uk_in, w_uv_in, w_value, kv, cut, attn, value,
    qn, qr, w_uk, w_uv, held, q_all, accum, top, total, x_sums, z_sums,
    y_send, y_recv, z_send, z_recv, c_send, c_recv, v_send, v_recv, in_sem,
):
    rows = qn.shape[0]
    heads, _, latent = w_uk.shape
    rope = qr.shape[1] // heads
    seq, head = lax.axis_index("seq"), lax.axis_index("head")
    core = lax.rem(seq, 2)
    y = lax.rem(lax.div(seq, 2), Y)
    z_lo = lax.div(seq, 2 * Y)
    x, z_hi = lax.div(head, Z_HI), lax.rem(head, Z_HI)

    def at_y(step):
        return ((z_lo * Y + lax.rem(y + step + Y, Y)) * 2 + core, head)

    other_plane = seq + (1 - 2 * z_lo) * 2 * Y
    z_up = (other_plane, x * Z_HI + lax.rem(z_hi + z_lo, Z_HI))
    z_down = (other_plane, x * Z_HI + lax.rem(z_hi + z_lo + Z_HI - 1, Z_HI))
    twin = (seq + 1 - 2 * core, head)
    y_to = (at_y(1), at_y(-1))
    z_to = (z_up, z_down)
    x_peers = [(seq, lax.rem(x + k, X) * Z_HI + z_hi) for k in range(1, X)]
    z_peers = [(seq, x * Z_HI + lax.rem(z_hi + k, Z_HI)) for k in range(1, Z_HI)]

    barrier = pltpu.get_barrier_semaphore()
    hand_to = (twin, (twin[0], x_peers[0][1]), twin, (twin[0], x_peers[X - 2][1]))
    greeted = [*y_to, *z_to, *hand_to[1:], *x_peers, *z_peers]
    for device in greeted:
        pl.semaphore_signal(barrier, inc=1, device_id=device, device_id_type=MESH)

    part_depth = kv.shape[0] // 2

    def place(slot, half=None):
        if half is None:
            return held.at[slot * 2 + core]
        return held.at[slot * 2 + core, pl.ds(half * part_depth, part_depth)]

    def own(half):
        return kv.at[pl.ds(half * part_depth, part_depth)]

    def half_of(stream, unit):
        return unit % 2 if stream == 0 else 1 - unit % 2

    def away(stream, steps):
        return steps if stream == 0 else (Y - steps) % Y

    def y_copy(stream, unit):
        steps, half = unit // 2, half_of(stream, unit)
        source = own(half) if steps == 0 else place(chip_slot(0, away(stream, steps)), half)
        return pltpu.make_async_remote_copy(
            src_ref=source,
            dst_ref=place(chip_slot(0, away(stream, steps + 1)), half),
            send_sem=y_send.at[stream, unit],
            recv_sem=y_recv.at[stream, unit],
            device_id=y_to[stream],
            device_id_type=MESH,
        )

    def z_copy(stream, unit):
        if unit == 0:
            steps, half = 0, stream
            source = own(half)
        else:
            steps, half = (unit - 1) // 2 + 1, half_of(stream, unit - 1)
            source = place(chip_slot(0, away(stream, steps)), half)
        return pltpu.make_async_remote_copy(
            src_ref=source,
            dst_ref=place(chip_slot(1, away(stream, steps)), half),
            send_sem=z_send.at[stream, unit],
            recv_sem=z_recv.at[stream, unit],
            device_id=z_to[stream],
            device_id_type=MESH,
        )

    def twin_copy(index):
        if index == 0:
            source, target = kv, place(chip_slot(0, 0))
        else:
            if index < 15:
                stream, unit = (index - 1) % 2, (index - 1) // 2
                slot, half = chip_slot(0, away(stream, unit // 2 + 1)), half_of(stream, unit)
            else:
                stream, unit = (index - 15) % 2, (index - 15) // 2
                if unit == 0:
                    slot, half = chip_slot(1, 0), stream
                else:
                    slot = chip_slot(1, away(stream, (unit - 1) // 2 + 1))
                    half = half_of(stream, unit - 1)
            source = target = place(slot, half)
        return pltpu.make_async_remote_copy(
            src_ref=source,
            dst_ref=target,
            send_sem=c_send.at[index],
            recv_sem=c_recv.at[index],
            device_id=hand_to[index % 4],
            device_id_type=MESH,
        )

    def from_y(unit):
        for stream in range(2):
            y_copy(stream, unit).wait_recv()
            if unit + 2 < 7:
                y_copy(stream, unit + 2).start()
            z_copy(stream, unit + 1).start()
            twin_copy(1 + unit * 2 + stream).start()

    def from_z(unit):
        for stream in range(2):
            z_copy(stream, unit).wait_recv()
            twin_copy(15 + unit * 2 + stream).start()

    def from_twin(*indices):
        for index in indices:
            twin_copy(index).wait_recv()


    def first_event(plane, steps):
        z_at = lax.rem(z_lo + plane, 2)
        return (z_at * Y + lax.rem(y - steps + Y, Y)) * CHIP

    def attend(pair):
        if pair == 0:
            chips = ((0, 0), (1, 0))
        elif pair == 7:
            chips = ((0, 4), (1, 4))
        else:
            steps, plane = (pair - 1) // 2 + 1, (pair - 1) % 2
            chips = ((plane, steps), (plane, Y - steps))
        first, second = first_event(*chips[0]), first_event(*chips[1])
        size = 2 * CHIP
        column = lax.broadcasted_iota(jnp.int32, (rows, size), 1)
        event = column + jnp.where(column < CHIP, first, second - CHIP)
        bias = jnp.where(event < visible, 0.0, HIDDEN)
        block = jnp.concatenate([held[pair * 4 + k] for k in range(4)], axis=1)
        per = heads // BLOCKS
        for part in range(BLOCKS):
            span = pl.ds(part * per * rows, per * rows)
            score = jnp.dot(q_all[span, :], block, preferred_element_type=jnp.float32)
            weights, scales = [], []
            for h in range(per):
                mine = pl.ds((part * per + h) * rows, rows)
                s = score[h * rows : (h + 1) * rows, :] + bias
                newest = jnp.max(s, axis=1, keepdims=True)
                if pair > 0:
                    newest = jnp.maximum(newest, top[mine, 0:1])
                    scale = jnp.exp2((top[mine, 0:1] - newest) * exp2_scale)
                    scales.append(scale)
                w = jnp.exp2((s - newest) * exp2_scale)
                added = sum(w[:, k : k + 128] for k in range(128, size, 128)) + w[:, :128]
                total[mine, :] = added if pair == 0 else total[mine, :] * scale + added
                top[mine, :] = jnp.broadcast_to(newest, (rows, 128))
                weights.append(w.astype(jnp.bfloat16))
            update = lax.dot_general(
                jnp.concatenate(weights, axis=0), block[:latent], (((1,), (1,)), ((), ())),
                preferred_element_type=jnp.float32,
            )
            if pair == 0:
                accum[span, :] = update
            else:
                accum[span, :] = accum[span, :] * jnp.concatenate(scales, axis=0) + update

    fetches = [
        pltpu.make_async_copy(source, target, in_sem.at[k])
        for k, (source, target) in enumerate(
            ((qn_in, qn), (w_uk_in, w_uk), (qr_in, qr), (kv, place(chip_slot(0, 0))), (w_uv_in, w_uv))
        )
    ]
    for fetch in fetches:
        fetch.start()
    square = (rows, rows)
    on_diagonal = lax.broadcasted_iota(jnp.int32, square, 0) == lax.broadcasted_iota(jnp.int32, square, 1)
    as_row = jnp.broadcast_to(cut[...].astype(jnp.float32), square)
    visible = jnp.sum(jnp.where(on_diagonal, as_row, 0.0), axis=1, keepdims=True).astype(jnp.int32)

    pl.semaphore_wait(barrier, len(greeted))
    for unit in range(2):
        for stream in range(2):
            y_copy(stream, unit).start()
            if unit == 0:
                z_copy(stream, 0).start()
    twin_copy(0).start()

    for fetch in fetches[:3]:
        fetch.wait()
    for h in range(heads):
        mine = pl.ds(h * rows, rows)
        q_lat = jnp.dot(qn[:, h * 128 : (h + 1) * 128], w_uk[h], preferred_element_type=jnp.float32)
        q_all[mine, :latent] = q_lat.astype(jnp.bfloat16)
        q_all[mine, latent:] = qr[:, h * rope : (h + 1) * rope]

    from_y(0)
    from_z(0)
    from_y(1)
    fetches[3].wait()
    from_twin(0, 15, 16)
    attend(0)
    from_y(2)
    from_z(1)
    from_z(2)
    from_twin(1, 2, 3, 4)
    attend(1)
    from_y(3)
    from_twin(17, 18, 19, 20)
    attend(2)
    from_y(4)
    from_z(3)
    from_z(4)
    from_twin(5, 6, 7, 8)
    attend(3)
    from_y(5)
    from_twin(21, 22, 23, 24)
    attend(4)
    from_y(6)
    from_z(5)
    from_z(6)
    from_twin(9, 10, 11, 12)
    attend(5)
    from_z(7)
    from_twin(25, 26, 27, 28)
    attend(6)
    from_twin(13, 14, 29, 30)
    attend(7)

    fetches[4].wait()
    share = jnp.zeros((rows, 128), jnp.float32)
    for h in range(heads):
        mine = pl.ds(h * rows, rows)
        inverse = 1.0 / jnp.sum(total[mine, :], axis=1, keepdims=True)
        o_lat = (accum[mine, :] * inverse).astype(jnp.bfloat16)
        out = jnp.dot(o_lat, w_uv[h], preferred_element_type=jnp.float32).astype(jnp.bfloat16)
        attn[:, h * 128 : (h + 1) * 128] = out
        share = share + out.astype(jnp.float32) * w_value[h : h + 1, :]
    partial = lax.dot_general(
        jnp.ones((8, 128), jnp.float32), share, (((1,), (1,)), ((), ())),
        precision=lax.Precision.HIGHEST, preferred_element_type=jnp.float32,
    )

    def exchange(stage, sums, peers, place_here, count, mine):
        sums[0, :, :rows] = mine
        copies = [
            pltpu.make_async_remote_copy(
                src_ref=sums.at[0],
                dst_ref=sums.at[k],
                send_sem=v_send.at[stage, k],
                recv_sem=v_recv.at[stage, k],
                device_id=peers[k - 1],
                device_id_type=MESH,
            )
            for k in range(1, count)
        ]
        for copy in copies:
            copy.start()
        for copy in copies:
            copy.wait()
        result = sums[place_here, :, :rows]
        for j in range(1, count):
            result = result + sums[lax.rem(place_here - j + count, count), :, :rows]
        return result

    along_x = exchange(0, x_sums, x_peers, x, X, partial)
    value[...] = exchange(1, z_sums, z_peers, z_hi, Z_HI, along_x)[:1]

    for stream in range(2):
        for unit in range(7):
            y_copy(stream, unit).wait_send()
        for unit in range(8):
            z_copy(stream, unit).wait_send()
    for index in range(31):
        twin_copy(index).wait_send()


def on_device(q_nope, q_rope, w_uk, w_uv, w_value, kv_cache, cutoffs):
    rows = q_nope.shape[0]
    heads, _, latent = w_uk.shape
    depth = kv_cache.shape[1]
    place = pl.BlockSpec(memory_space=pl.ANY)
    vmem = pl.BlockSpec(memory_space=pltpu.VMEM)
    dma = pltpu.SemaphoreType.DMA
    attn, value = pl.pallas_call(
        kernel,
        out_shape=(
            jax.ShapeDtypeStruct((rows, q_nope.shape[1]), jnp.bfloat16),
            jax.ShapeDtypeStruct((1, rows), jnp.float32),
        ),
        in_specs=[place] * 4 + [vmem, place, vmem],
        out_specs=(vmem, vmem),
        scratch_shapes=[
            pltpu.VMEM(q_nope.shape, jnp.bfloat16),
            pltpu.VMEM(q_rope.shape, jnp.bfloat16),
            pltpu.VMEM(w_uk.shape, jnp.bfloat16),
            pltpu.VMEM(w_uv.shape, jnp.bfloat16),
            pltpu.VMEM((32, depth, SHARD), jnp.bfloat16),
            pltpu.VMEM((heads * rows, depth), jnp.bfloat16),
            pltpu.VMEM((heads * rows, latent), jnp.float32),
            pltpu.VMEM((heads * rows, 128), jnp.float32),
            pltpu.VMEM((heads * rows, 128), jnp.float32),
            pltpu.VMEM((X, 8, 128), jnp.float32),
            pltpu.VMEM((Z_HI, 8, 128), jnp.float32),
            dma((2, 7)), dma((2, 7)), dma((2, 8)), dma((2, 8)), dma((31,)), dma((31,)),
            dma((2, 4)), dma((2, 4)), dma((5,)),
        ],
        compiler_params=pltpu.CompilerParams(
            collective_id=0, has_side_effects=True, vmem_limit_bytes=60 * 2**20
        ),
    )(q_nope, q_rope, w_uk, w_uv, w_value.reshape(heads, -1), kv_cache.T, cutoffs.reshape(1, rows))
    return attn, value.reshape(rows)


def solution(mesh):
    placed = (
        P("seq", "head"),
        P("seq", "head"),
        P("head", None, None),
        P("head", None, None),
        P("head"),
        P("seq", None),
        P("seq"),
    )
    return jax.shard_map(
        on_device,
        mesh=mesh,
        in_specs=placed,
        out_specs=(P("seq", "head"), P("seq")),
        check_vma=False,
    )
```
